32 devices in a mesh: dp: 8 (over z, y), seq: 4 (over x, core).
Axes of the slice: x: 2, y: 2, z: 4, core: 2. Of those that a mesh axis runs over, the one named last changes fastest.
Arguments:
- block_input: bfloat16 [8, 512, 1024], P('dp', 'seq'), may hold values from -6 to 6
- in_weight: bfloat16 [1024, 4384], P(('dp', 'seq')), may hold values from -0.1875 to 0.1875
- out_weight: bfloat16 [2048, 1024], P(None, ('dp', 'seq')), may hold values from -0.125 to 0.125
- pre_gain: bfloat16 [1024], P(('dp', 'seq')), may hold values from 0.099609375 to 1.8984375
- norm_gain: bfloat16 [2048], P(('dp', 'seq')), may hold values from 0.099609375 to 1.8984375
- conv_weight: bfloat16 [4, 2304], P(None, ('dp', 'seq')), may hold values from -3 to 3
- conv_bias: bfloat16 [2304], P(('dp', 'seq')), may hold values from -1.5 to 1.5
- dt_bias: float32 [32], replicated, may hold values from -11 to -2, as said below
- decay_log: float32 [32], replicated, may hold values from 0 to 1
- skip_gain: float32 [32], replicated, may hold values from 0.5 to 1.5
- cotangent: bfloat16 [8, 512, 1024], P('dp', 'seq'), may hold values from -6 to 6
Outputs:
- block_output: bfloat16 [8, 512, 1024], P('dp', 'seq')
- input_grad: float32 [8, 512, 1024], P('dp', 'seq')
- in_weight_grad: float32 [1024, 4384], P(('dp', 'seq'))
- out_weight_grad: float32 [2048, 1024], P(None, ('dp', 'seq'))
- pre_gain_grad: float32 [1024], P(('dp', 'seq'))
- norm_gain_grad: float32 [2048], P(('dp', 'seq'))
- conv_weight_grad: float32 [4, 2304], P(None, ('dp', 'seq'))
- conv_bias_grad: float32 [2304], P(('dp', 'seq'))
- dt_bias_grad: float32 [32], replicated
- decay_log_grad: float32 [32], replicated
- skip_gain_grad: float32 [32], replicated
The draws below stay inside these ranges and needn't reach their ends.
Inputs may be any that keep to these rules, and one draw needn't show every extreme that they name: `dt_bias`: each head's bias is a float between -11 and -2.
All inputs are finite; a program needn't handle non-finite values.
Results may differ from the reference program's by a relative error of at most 0.0067.
Values may be sent and summed in bfloat16 or wider, within the bound.
A program may use at most 256 MiB of HBM per device.

```python
import jax
import jax.numpy as jnp
from jax import lax

D = 1024
HEADS = 32
HEAD_DIM = 64
STATE = 128
CONV = 4
GROUP = 128
INNER = 2048
CONV_CH = 2304
PROJ = 4384
SEQS = 8
LENGTH = 512


def draw_dt_bias(key, part):
    key_order, key_slow, key_fast = jax.random.split(jax.random.fold_in(key, 11), 3)
    order = jax.random.permutation(key_order, HEADS)
    slow_count = HEADS // 2
    slow_values = jnp.log(jax.random.uniform(key_slow, (HEADS,), jnp.float32, 0.05, 0.3) / LENGTH)
    fast_values = jax.random.uniform(key_fast, (HEADS,), jnp.float32, -4.0, -2.5)
    return jnp.where(order < slow_count, slow_values, fast_values).astype(jnp.float32)


def with_spikes(entries, stream_key, source, target, shards_of, factor):
    owner, partner = [(jnp.arange(entries.shape[dim]) // (entries.shape[dim] // shards_of)).reshape([-1 if axis == dim else 1 for axis in range(entries.ndim)]) for dim in (source, target)]
    chosen = jax.random.permutation(stream_key, shards_of)[partner]
    strong = (owner == chosen) | (owner == (partner + shards_of // 2) % shards_of)
    return jnp.where(strong, factor * entries, entries)


def levels(rng, dims, cuts, least, high):
    factor_of = 1.0
    for dim, parts in cuts:
        steps = jax.random.uniform(jax.random.fold_in(jax.random.fold_in(rng, 6), dim), (parts,), jnp.float32, least / len(cuts), high / len(cuts))
        factor_of = factor_of * jnp.repeat(jnp.exp(steps), dims[dim] // parts).reshape((-1,) + (1,) * (len(dims) - 1 - dim))
    return factor_of


def scatter_about(own_key, extent, scale, reach, cuts=(), dtype=jnp.bfloat16):
    factor_of = levels(own_key, extent, cuts, -0.22, 0.18) if cuts else 1.0
    entries = jax.random.normal(own_key, extent, jnp.float32) * scale * factor_of
    return jnp.minimum(jnp.maximum(entries, -reach), reach).astype(dtype)


def heavy_noise(stream_key, shape, scale, most, pieces, heavy, kind=jnp.bfloat16):
    array = scale * jax.random.normal(stream_key, shape, jnp.float32)
    if pieces:
        array = array * levels(stream_key, shape, pieces, -0.22, 0.18)
    return jnp.clip(with_spikes(array, jax.random.fold_in(stream_key, 3), *heavy), -most, most).astype(kind)


def setup_inputs(seed: int = 0) -> dict:
    arg_keys = jax.random.split(jax.random.key(seed), 12)
    return {
        "block_input": heavy_noise(arg_keys[0], (SEQS, LENGTH, D), 1.0, 6.0, ((0, 8), (1, 4)), (0, 2, 8, 2.0)),
        "in_weight": scatter_about(arg_keys[1], (D, PROJ), D ** -0.5, 0.1875, ((0, 32),)),
        "out_weight": scatter_about(arg_keys[2], (INNER, D), INNER ** -0.5, 0.125, ((1, 32),)),
        "pre_gain": jnp.clip(1.0 + 0.18 * jax.random.normal(arg_keys[3], (D,), jnp.float32), 0.099609375, 1.8984375).astype(jnp.bfloat16),
        "norm_gain": jnp.clip(1.0 + 0.18 * jax.random.normal(arg_keys[4], (INNER,), jnp.float32), 0.099609375, 1.8984375).astype(jnp.bfloat16),
        "conv_weight": scatter_about(arg_keys[5], (CONV, CONV_CH), CONV ** -0.5, 3.0, ((1, 32),)),
        "conv_bias": scatter_about(arg_keys[6], (CONV_CH,), 0.3, 1.5, ((0, 32),)),
        "dt_bias": draw_dt_bias(jax.random.fold_in(arg_keys[11], 71), 0),
        "decay_log": jnp.clip(jax.random.uniform(arg_keys[8], (HEADS,), jnp.float32, 0.0, 1.0), 0.0, 1.0),
        "skip_gain": jnp.clip(jax.random.uniform(arg_keys[9], (HEADS,), jnp.float32, 0.5, 1.5), 0.5, 1.5),
        "cotangent": heavy_noise(arg_keys[10], (SEQS, LENGTH, D), 1.0, 6.0, ((0, 8), (1, 4)), (0, 2, 8, 2.0)),
    }


epsilon = 1e-05
highest = lax.Precision.HIGHEST

def convolve(padded, conv_weight, conv_bias):
    taps = conv_weight.shape[0]
    length = padded.shape[-2] - taps + 1
    total = conv_bias
    for index in range(taps):
        total = total + conv_weight[index] * lax.slice_in_dim(padded, index, index + length, axis=padded.ndim - 2)
    return total

def front(projected, rim, conv_weight, conv_bias, dt_bias, decay_log):
    gate_raw = projected[..., :INNER]
    conv_in = projected[..., INNER:INNER + CONV_CH]
    dt_raw = projected[..., INNER + CONV_CH:]
    padded = jnp.concatenate([rim, conv_in], axis=-2)
    conv_out = jax.nn.silu(convolve(padded, conv_weight, conv_bias))
    values = conv_out[..., :INNER]
    in_map = conv_out[..., INNER:INNER + STATE]
    out_map = conv_out[..., INNER + STATE:]
    step = jax.nn.softplus(dt_raw + dt_bias)
    return (gate_raw, values, in_map, out_map, step)

def group_state(values, in_map, step, cumulative):
    weights_end = jnp.exp(cumulative[-1][None, :] - cumulative) * step
    state = jnp.einsum('shp,sn->hpn', values * weights_end[:, :, None], in_map, precision=highest)
    return (state, jnp.exp(cumulative[-1]))

def group_output(values, in_map, out_map, step, cumulative, carried, skip_gain):
    length = values.shape[0]
    scores = jnp.dot(out_map, in_map.T, precision=highest)
    causal = jnp.arange(length)[:, None] >= jnp.arange(length)[None, :]
    spread = cumulative[:, None, :] - cumulative[None, :, :]
    decay = jnp.exp(jnp.where(causal[:, :, None], spread, -10000.0))
    mixing = scores[:, :, None] * decay * step[None, :, :]
    inner_part = jnp.einsum('tsh,shp->thp', mixing, values, precision=highest)
    carried_part = jnp.einsum('tn,hpn->thp', out_map, carried, precision=highest) * jnp.exp(cumulative)[:, :, None]
    return inner_part + carried_part + skip_gain[None, :, None] * values

def gate_norm(ssd_out, gate_raw, norm_gain):
    gated = ssd_out * jax.nn.silu(gate_raw)
    inverse = lax.rsqrt(lax.optimization_barrier(jnp.mean(gated * gated, axis=-1, keepdims=True)) + epsilon)
    return gated * inverse * norm_gain

def middle(projected, conv_weight, conv_bias, dt_bias, decay_log, skip_gain, norm_gain):
    length = projected.shape[0]
    rim = jnp.zeros((CONV - 1, CONV_CH), jnp.float32)
    gate_raw, values, in_map, out_map, step = front(projected, rim, conv_weight, conv_bias, dt_bias, decay_log)
    groups = length // GROUP
    values = values.reshape(groups, GROUP, HEADS, HEAD_DIM)
    in_map = in_map.reshape(groups, GROUP, STATE)
    out_map = out_map.reshape(groups, GROUP, STATE)
    step = step.reshape(groups, GROUP, HEADS)
    cumulative = jnp.cumsum(step * -jnp.exp(decay_log), axis=1)
    states, decays = jax.vmap(group_state)(values, in_map, step, cumulative)

    def carry_step(carry, pair):
        decay_now, state_now = pair
        return (decay_now[:, None, None] * carry + state_now, carry)
    start = jnp.zeros((HEADS, HEAD_DIM, STATE), jnp.float32)
    unused, carried = lax.scan(carry_step, start, (decays, states))
    ssd_out = jax.vmap(group_output, in_axes=(0, 0, 0, 0, 0, 0, None))(values, in_map, out_map, step, cumulative, carried, skip_gain)
    return gate_norm(ssd_out.reshape(length, INNER), gate_raw, norm_gain)

def reference(block_input, in_weight, out_weight, pre_gain, norm_gain, conv_weight, conv_bias, dt_bias, decay_log, skip_gain, cotangent):
    pre_float = pre_gain.astype(jnp.float32)
    norm_float = norm_gain.astype(jnp.float32)
    conv_w_float = conv_weight.astype(jnp.float32)
    conv_b_float = conv_bias.astype(jnp.float32)

    def one_sequence(totals, pair):
        block, grad_out = pair
        inputs = block.astype(jnp.float32)
        inv_pre = lax.rsqrt(lax.optimization_barrier(jnp.mean(inputs * inputs, axis=-1, keepdims=True)) + epsilon)
        normed = (inputs * inv_pre * pre_float).astype(jnp.bfloat16)
        projected = jnp.dot(normed, in_weight, preferred_element_type=jnp.float32)
        mixed_float, pullback = jax.vjp(middle, projected, conv_w_float, conv_b_float, dt_bias, decay_log, skip_gain, norm_float)
        mixed = mixed_float.astype(jnp.bfloat16)
        output = (inputs + jnp.dot(mixed, out_weight, preferred_element_type=jnp.float32)).astype(jnp.bfloat16)
        mixed_grad = jnp.dot(grad_out, out_weight.T, preferred_element_type=jnp.float32)
        out_w_grad = jnp.dot(mixed.T, grad_out, preferred_element_type=jnp.float32)
        proj_float, conv_w_grad, conv_b_grad, dt_grad, decay_grad, skip_grad, norm_grad = pullback(mixed_grad)
        proj_grad = proj_float.astype(jnp.bfloat16)
        in_w_grad = jnp.dot(normed.T, proj_grad, preferred_element_type=jnp.float32)
        normed_grad = jnp.dot(proj_grad, in_weight.T, preferred_element_type=jnp.float32)
        pre_grad = lax.optimization_barrier(jnp.sum(normed_grad * inputs * inv_pre, axis=0))
        scaled = normed_grad * pre_float
        unit = inputs * inv_pre
        input_grad = inv_pre * (scaled - unit * lax.optimization_barrier(jnp.mean(scaled * unit, axis=-1, keepdims=True))) + grad_out.astype(jnp.float32)
        terms = (in_w_grad, out_w_grad, pre_grad, norm_grad, conv_w_grad, conv_b_grad, dt_grad, decay_grad, skip_grad)
        totals = tuple((total + term for total, term in zip(totals, terms)))
        return (totals, (output, input_grad))
    zeros = (jnp.zeros((D, PROJ), jnp.float32), jnp.zeros((INNER, D), jnp.float32), jnp.zeros((D,), jnp.float32), jnp.zeros((INNER,), jnp.float32), jnp.zeros((CONV, CONV_CH), jnp.float32), jnp.zeros((CONV_CH,), jnp.float32), jnp.zeros((HEADS,), jnp.float32), jnp.zeros((HEADS,), jnp.float32), jnp.zeros((HEADS,), jnp.float32))
    totals, stacked = lax.scan(one_sequence, zeros, (block_input, cotangent))
    return (stacked[0], stacked[1], totals[0], totals[1], totals[2], totals[3], totals[4], totals[5], totals[6], totals[7], totals[8])
```

```python
import functools

import jax
import jax.numpy as jnp
from jax import lax
from jax.experimental import pallas as pl
from jax.experimental.pallas import tpu as pltpu
from jax.sharding import PartitionSpec as P

HEADS = 32
HEAD_DIM = 64
STATE = 128
CONV = 4
INNER = 2048
CONV_CH = 2304


epsilon = 1e-05
highest = lax.Precision.HIGHEST


def from_behind(value, axis, steps):
    count = lax.axis_size(axis)
    leading, last = (max(0, -steps), min(count, count - steps))
    return lax.ppermute(value, axis, [(source, source + steps) for source in range(leading, last)])


def convolve(padded, conv_weight, conv_bias):
    taps = conv_weight.shape[0]
    length = padded.shape[-2] - taps + 1
    total = conv_bias
    for index in range(taps):
        total = total + conv_weight[index] * lax.slice_in_dim(
            padded, index, index + length, axis=padded.ndim - 2
        )
    return total


def bits_of(count):
    return count.bit_length() - 1


def can_pair(shapes, rows):
    return all(size & (size - 1) == 0 for size in shapes) and rows % 16 == 0


def bit_orders(total):
    first, rest = [0], list(range(1, total))
    turned = rest[1:] + rest[:1]
    third = rest[2:3] + rest[:2] + rest[3:]
    return [first + rest, first + turned, first + third, first + rest]


class Place:
    def __init__(self, dp, seq):
        self.dp, self.seq = lax.axis_index("dp"), lax.axis_index("seq")
        self.low, self.total = bits_of(seq), bits_of(seq) + bits_of(dp)
        self.owner = self.dp * seq + self.seq

    def bit(self, b):
        return lax.rem(self.owner // 2**b, 2)

    def partner(self, b):
        step = 1 - 2 * self.bit(b)
        if b < self.low:
            return (self.dp, self.seq + step * 2**b)
        return (self.dp + step * 2 ** (b - self.low), self.seq)

    def flipped(self, pairs):
        total = self.owner
        for b, flag in pairs:
            total = total + flag * (1 - 2 * self.bit(b)) * 2**b
        return total

    def greet(self):
        barrier = pltpu.get_barrier_semaphore()
        for b in range(self.total):
            pl.semaphore_signal(
                barrier, inc=1, device_id=self.partner(b), device_id_type=pl.DeviceIdType.MESH
            )
        pl.semaphore_wait(barrier, self.total)


def remote(src, dst, send, recv, device):
    return pltpu.make_async_remote_copy(
        src_ref=src,
        dst_ref=dst,
        send_sem=send,
        recv_sem=recv,
        device_id=device,
        device_id_type=pl.DeviceIdType.MESH,
    )


def gather_kernel(dp, seq, count, *refs):
    ins, outs = refs[:count], refs[count : 2 * count]
    send, recv, own = refs[2 * count :]
    place = Place(dp, seq)
    n = place.total
    orders = [order[::-1] for order in bit_orders(n)]
    locals_ = []
    for s in range(count):
        copy = pltpu.make_async_copy(ins[s], outs[s].at[place.owner], own.at[s])
        copy.start()
        locals_.append(copy)
    place.greet()

    def copy_of(s, held, src, stage):
        order = orders[s]
        owner = place.flipped([(order[i], lax.rem(held // 2**i, 2)) for i in range(stage)])
        slot = 2**stage - 1 + held
        source = src if src is not None else outs[s].at[owner]
        return remote(
            source, outs[s].at[owner], send.at[s, slot], recv.at[s, slot], place.partner(order[stage])
        )

    for stage in range(n - 1, -1, -1):
        for s in range(count):
            copy_of(s, 0, ins[s], stage).start()
    for stage in range(n):

        def arrived(j, carry, stage=stage):
            for s in range(count):
                copy_of(s, j, None, stage).wait_recv()
                for later in range(n - 1, stage, -1):
                    copy_of(s, 2**stage + j, None, later).start()
            return carry

        lax.fori_loop(0, 2**stage, arrived, 0)
    for stage in range(n):

        def sent(j, carry, stage=stage):
            for s in range(count):
                copy_of(s, j, None, stage).wait_send()
            return carry

        lax.fori_loop(0, 2**stage, sent, 0)
    for copy in locals_:
        copy.wait()


def gather_blocks(blocks, dp, seq):
    count, owners = len(blocks), dp * seq
    return pl.pallas_call(
        functools.partial(gather_kernel, dp, seq, count),
        out_shape=[jax.ShapeDtypeStruct((owners,) + b.shape, b.dtype) for b in blocks],
        in_specs=[pl.BlockSpec(memory_space=pltpu.VMEM)] * count,
        out_specs=[pl.BlockSpec(memory_space=pltpu.VMEM)] * count,
        scratch_shapes=[
            pltpu.SemaphoreType.DMA((count, owners)),
            pltpu.SemaphoreType.DMA((count, owners)),
            pltpu.SemaphoreType.DMA((count,)),
        ],
        compiler_params=pltpu.CompilerParams(
            collective_id=0, has_side_effects=True, vmem_limit_bytes=56 * 2**20
        ),
    )(*blocks)


def reduce_kernel(dp, seq, count, *refs):
    ins, outs = refs[:count], refs[count : 2 * count]
    boxes, sums = refs[2 * count : 3 * count], refs[3 * count : 4 * count]
    send, recv = refs[4 * count :]
    place = Place(dp, seq)
    n = place.total
    half0 = 2 ** (n - 1)
    orders = bit_orders(n)
    place.greet()

    def block_of(s, j, mine):
        order = orders[s]
        pairs = [(order[i], 1 - lax.rem(j // 2 ** (n - 1 - i), 2)) for i in range(1, n)]
        return place.flipped(pairs + [(order[0], 0 if mine else 1)])

    def copy_of(s, j, stage):
        half = half0 // 2**stage
        slot = 2 * half0 - 2 * half + j
        if stage == 0:
            source = ins[s].at[block_of(s, j, False)]
        else:
            source = sums[s].at[half0 - 2 * half + j]
        return remote(
            source,
            boxes[s].at[slot],
            send.at[s, slot],
            recv.at[s, slot],
            place.partner(orders[s][stage]),
        )

    def begin(j, carry):
        for s in range(count):
            copy_of(s, j, 0).start()
        return carry

    lax.fori_loop(0, half0, begin, 0)
    for stage in range(n):
        half = half0 // 2**stage

        def add(s, j, stage, half):
            slot = 2 * half0 - 2 * half + j
            here = half0 - half + j
            rows, columns = outs[s].shape
            wide = 512 if columns > 512 else columns
            for start in range(0, columns, wide):
                part = pl.ds(start, min(wide, columns - start))
                if stage == 0:
                    kept = ins[s][block_of(s, j, True), :, part]
                else:
                    kept = sums[s][here, :, part]
                total = kept.astype(jnp.float32) + boxes[s][slot, :, part].astype(jnp.float32)
                if stage == n - 1:
                    outs[s][:, part] = total
                else:
                    sums[s][here, :, part] = total.astype(sums[s].dtype)

        def forward(j, carry, stage=stage, half=half):
            for s in range(count):
                copy_of(s, j, stage).wait_recv()
                add(s, j, stage, half)
                copy_of(s, j, stage + 1).start()
            return carry

        def keep(j, carry, stage=stage, half=half):
            for s in range(count):
                copy_of(s, j, stage).wait_recv()
                add(s, j, stage, half)
            return carry

        if stage < n - 1:
            lax.fori_loop(0, half // 2, forward, 0)
            lax.fori_loop(half // 2, half, keep, 0)
        else:
            keep(0, 0)
    for stage in range(n):

        def sent(j, carry, stage=stage):
            for s in range(count):
                copy_of(s, j, stage).wait_send()
            return carry

        lax.fori_loop(0, half0 // 2**stage, sent, 0)


def reduce_blocks(blocks, dp, seq):
    count, owners = len(blocks), dp * seq
    return pl.pallas_call(
        functools.partial(reduce_kernel, dp, seq, count),
        out_shape=[jax.ShapeDtypeStruct(b.shape[1:], jnp.float32) for b in blocks],
        in_specs=[pl.BlockSpec(memory_space=pltpu.VMEM)] * count,
        out_specs=[pl.BlockSpec(memory_space=pltpu.VMEM)] * count,
        scratch_shapes=[pltpu.VMEM(b.shape, b.dtype) for b in blocks]
        + [pltpu.VMEM((owners // 2,) + b.shape[1:], b.dtype) for b in blocks]
        + [pltpu.SemaphoreType.DMA((count, owners)), pltpu.SemaphoreType.DMA((count, owners))],
        compiler_params=pltpu.CompilerParams(
            collective_id=1, has_side_effects=True, vmem_limit_bytes=58 * 2**20
        ),
    )(*blocks)


def carry_scan(state, decay, axis, sign):
    count = lax.axis_size(axis)
    within, within_decay = state, decay
    entering, entering_decay = None, None
    width = 1
    while width < count:
        moved = from_behind(within.astype(jnp.bfloat16), axis, sign * width).astype(jnp.float32)
        last = 2 * width >= count
        if not last or entering is None:
            moved_decay = from_behind(within_decay, axis, sign * width)
        if entering is None:
            entering, entering_decay = moved, moved_decay
        else:
            entering = entering + entering_decay[:, :, None, None] * moved
            if not last:
                entering_decay = entering_decay * moved_decay
        if not last:
            within = within + within_decay[:, :, None, None] * moved
            within_decay = within_decay * moved_decay
        width *= 2
    return jnp.zeros_like(state) if entering is None else entering


def front_fn(tail, rim, conv_weight, conv_bias, dt_bias, decay_log):
    conv_in = tail[..., :CONV_CH]
    dt_raw = tail[..., CONV_CH:]
    padded = jnp.concatenate([rim, conv_in], axis=-2)
    conv_out = jax.nn.silu(convolve(padded, conv_weight, conv_bias))
    leading = conv_out.shape[:-1]
    values = conv_out[..., :INNER].reshape(leading + (HEADS, HEAD_DIM))
    in_map = conv_out[..., INNER : INNER + STATE]
    out_map = conv_out[..., INNER + STATE :]
    step = jax.nn.softplus(dt_raw + dt_bias)
    cumulative = jnp.cumsum(step * -jnp.exp(decay_log), axis=1)
    return (values, in_map, out_map, step, cumulative)


def group_state(values, in_map, step, cumulative):
    weights_end = jnp.exp(cumulative[-1][None, :] - cumulative) * step
    state = jnp.einsum("shp,sn->hpn", values * weights_end[:, :, None], in_map, precision=highest)
    return (state, jnp.exp(cumulative[-1]))


def group_output(values, in_map, out_map, step, cumulative, carried, skip_gain):
    length = values.shape[0]
    scores = jnp.dot(out_map, in_map.T, precision=highest)
    causal = jnp.arange(length)[:, None] >= jnp.arange(length)[None, :]
    spread = cumulative[:, None, :] - cumulative[None, :, :]
    decay = jnp.exp(jnp.where(causal[:, :, None], spread, -10000.0))
    mixing = scores[:, :, None] * decay * step[None, :, :]
    inner_part = jnp.einsum("tsh,shp->thp", mixing, values, precision=highest)
    carried_part = (
        jnp.einsum("tn,hpn->thp", out_map, carried, precision=highest)
        * jnp.exp(cumulative)[:, :, None]
    )
    return inner_part + carried_part + skip_gain[None, :, None] * values


def state_fn(values, in_map, step, cumulative):
    return jax.vmap(group_state)(values, in_map, step, cumulative)


def out_fn(values, in_map, out_map, step, cumulative, gate_raw, carried, skip_gain, norm_gain):
    ssd_out = jax.vmap(group_output, in_axes=(0, 0, 0, 0, 0, 0, None))(
        values, in_map, out_map, step, cumulative, carried, skip_gain
    )
    ssd_out = ssd_out.reshape(gate_raw.shape)
    gated = ssd_out * jax.nn.silu(gate_raw)
    inverse = lax.rsqrt(jnp.mean(gated * gated, axis=-1, keepdims=True) + epsilon)
    return gated * inverse * norm_gain


def by_rows(grad, owners):
    return grad.reshape(owners, -1)


def by_columns(grad, owners):
    rows = grad.shape[0]
    return jnp.transpose(grad.reshape(rows, owners, -1), (1, 0, 2)).reshape(owners, -1)


def on_device(
    block_input,
    in_weight,
    out_weight,
    pre_gain,
    norm_gain,
    conv_weight,
    conv_bias,
    dt_bias,
    decay_log,
    skip_gain,
    cotangent,
):
    seq_dev, length, width = block_input.shape
    dp, seq = lax.axis_size("dp"), lax.axis_size("seq")
    owners = dp * seq
    both = ("dp", "seq")
    fast = can_pair((dp, seq), in_weight.shape[0]) and dp * seq > 4
    small_parts = (pre_gain, norm_gain, conv_weight.reshape(-1), conv_bias)
    small_sizes = [part.size for part in small_parts]
    small = jnp.concatenate(small_parts)
    if fast:
        lines = -(-small.size // 2048) * 16
        small = jnp.pad(small, (0, lines * 128 - small.size)).reshape(lines, 128)
        gate_w, tail_w, out_t, small_all = gather_blocks(
            (in_weight[:, :INNER], in_weight[:, INNER:], out_weight.T, small), dp, seq
        )
        gate_w = gate_w.reshape(width, -1)
        tail_w = tail_w.reshape(width, -1)
        out_t = out_t.reshape(width, INNER)
        small_all = small_all.reshape(owners, -1)
    else:
        in_full = lax.all_gather(in_weight, both, axis=0, tiled=True)
        gate_w, tail_w = in_full[:, :INNER], in_full[:, INNER:]
        out_t = lax.all_gather(out_weight.T, both, axis=0, tiled=True)
        small_all = lax.all_gather(small, both, axis=0)
    pieces, start = [], 0
    for size in small_sizes:
        pieces.append(small_all[:, start : start + size])
        start += size
    pre_full, norm_full, conv_b_full = (pieces[i].reshape(-1) for i in (0, 1, 3))
    conv_w_full = jnp.transpose(pieces[2].reshape(owners, CONV, -1), (1, 0, 2)).reshape(CONV, -1)
    pre_float = pre_full.astype(jnp.float32)
    norm_float = norm_full.astype(jnp.float32)
    inputs = block_input.astype(jnp.float32)
    inv_pre = lax.rsqrt(jnp.mean(inputs * inputs, axis=-1, keepdims=True) + epsilon)
    normed = (inputs * inv_pre * pre_float).astype(jnp.bfloat16)
    flat_normed = normed.reshape(seq_dev * length, width)
    gate_raw = jnp.dot(flat_normed, gate_w, preferred_element_type=jnp.float32).reshape(
        seq_dev, length, -1
    )
    tail = jnp.dot(flat_normed, tail_w, preferred_element_type=jnp.float32).reshape(
        seq_dev, length, -1
    )
    conv_in = tail[:, length - (CONV - 1) :, :CONV_CH]
    rim = from_behind(conv_in, "seq", 1)
    front_out, front_pull = jax.vjp(
        front_fn,
        tail,
        rim,
        conv_w_full.astype(jnp.float32),
        conv_b_full.astype(jnp.float32),
        dt_bias,
        decay_log,
    )
    values, in_map, out_map, step, cumulative = front_out
    state_out, state_pull = jax.vjp(state_fn, values, in_map, step, cumulative)
    state, decay = state_out
    carried = carry_scan(state, decay, "seq", 1)
    mixed_float, out_pull = jax.vjp(
        out_fn, values, in_map, out_map, step, cumulative, gate_raw, carried, skip_gain, norm_float
    )
    mixed = mixed_float.astype(jnp.bfloat16)
    flat_mixed = mixed.reshape(seq_dev * length, INNER)
    block_output = (
        inputs
        + jnp.dot(flat_mixed, out_t.T, preferred_element_type=jnp.float32).reshape(
            seq_dev, length, width
        )
    ).astype(jnp.bfloat16)
    flat_grad = cotangent.reshape(seq_dev * length, width)
    mixed_grad = jnp.dot(flat_grad, out_t, preferred_element_type=jnp.float32).reshape(
        seq_dev, length, INNER
    )
    out_w_grad = jnp.dot(flat_grad.T, flat_mixed, preferred_element_type=jnp.float32)
    (
        values_a,
        in_map_a,
        out_map_grad,
        step_a,
        cumul_a,
        gate_grad,
        local_grad,
        skip_grad,
        norm_grad,
    ) = out_pull(mixed_grad)

    later_grad = carry_scan(local_grad, decay, "seq", -1)
    decay_grad = jnp.sum(later_grad * carried, axis=(2, 3))
    values_b, in_map_b, step_b, cumul_b = state_pull((later_grad, decay_grad))
    front_grads = front_pull(
        (
            values_a + values_b,
            in_map_a + in_map_b,
            out_map_grad,
            step_a + step_b,
            cumul_a + cumul_b,
        )
    )
    tail_float, rim_grad, conv_w_grad, conv_b_grad, dt_grad, decay_log_grad = front_grads
    returned = from_behind(rim_grad, "seq", -1)
    tail_float = tail_float + jnp.pad(returned, ((0, 0), (length - (CONV - 1), 0), (0, HEADS)))
    tail_grad = tail_float.astype(jnp.bfloat16).reshape(seq_dev * length, -1)
    gate_grad = gate_grad.astype(jnp.bfloat16).reshape(seq_dev * length, -1)
    gate_w_grad = jnp.dot(flat_normed.T, gate_grad, preferred_element_type=jnp.float32)
    tail_w_grad = jnp.dot(flat_normed.T, tail_grad, preferred_element_type=jnp.float32)
    normed_grad = (
        jnp.dot(gate_grad, gate_w.T, preferred_element_type=jnp.float32)
        + jnp.dot(tail_grad, tail_w.T, preferred_element_type=jnp.float32)
    ).reshape(seq_dev, length, width)
    pre_grad = jnp.sum(normed_grad * inputs * inv_pre, axis=(0, 1))
    scaled = normed_grad * pre_float
    unit = inputs * inv_pre
    input_grad = inv_pre * (
        scaled - unit * jnp.mean(scaled * unit, axis=-1, keepdims=True)
    ) + cotangent.astype(jnp.float32)
    small_grads = jnp.concatenate(
        (
            by_rows(pre_grad, owners),
            by_rows(norm_grad, owners),
            by_columns(conv_w_grad, owners),
            by_rows(conv_b_grad, owners),
        ),
        axis=1,
    )
    heads = jnp.concatenate((dt_grad, decay_log_grad, skip_grad))
    if fast:
        total = small_grads.shape[1] + heads.size
        lines = -(-total // 1024) * 8
        heads_all = jnp.broadcast_to(heads, (owners, heads.size))
        small_grads = jnp.concatenate((small_grads, heads_all), axis=1)
        small_grads = jnp.pad(small_grads, ((0, 0), (0, lines * 128 - total)))
        rows = width // owners
        gate_share, tail_share, out_share, small_share = reduce_blocks(
            (
                gate_w_grad.astype(jnp.bfloat16).reshape(owners, rows, -1),
                tail_w_grad.astype(jnp.bfloat16).reshape(owners, rows, -1),
                out_w_grad.astype(jnp.bfloat16).reshape(owners, rows, -1),
                small_grads.reshape(owners, lines, 128),
            ),
            dp,
            seq,
        )
        small_share = small_share.reshape(-1)
        heads = small_share[total - heads.size : total]
        in_share = jnp.concatenate((gate_share, tail_share), axis=1)
        out_share = out_share.T
    else:
        scatter = functools.partial(
            lax.psum_scatter, axis_name=both, scatter_dimension=0, tiled=True
        )
        in_share = scatter(jnp.concatenate((gate_w_grad, tail_w_grad), axis=1))
        out_share = scatter(out_w_grad).T
        small_share = scatter(small_grads)[0]
        heads = lax.psum(heads, both)
    shares, start = [], 0
    for size in small_sizes:
        shares.append(small_share[start : start + size])
        start += size
    pre_share, norm_share, conv_w_share, conv_b_share = shares
    conv_w_share = conv_w_share.reshape(CONV, -1)
    heads_total = (heads[:HEADS], heads[HEADS : 2 * HEADS], heads[2 * HEADS :])
    return (
        block_output,
        input_grad,
        in_share,
        out_share,
        pre_share,
        norm_share,
        conv_w_share,
        conv_b_share,
        heads_total[0],
        heads_total[1],
        heads_total[2],
    )


def solution(mesh):
    in_specs = (
        P("dp", "seq", None),
        P(("dp", "seq"), None),
        P(None, ("dp", "seq")),
        P(("dp", "seq")),
        P(("dp", "seq")),
        P(None, ("dp", "seq")),
        P(("dp", "seq")),
        P(),
        P(),
        P(),
        P("dp", "seq", None),
    )
    out_specs = (
        P("dp", "seq", None),
        P("dp", "seq", None),
        P(("dp", "seq"), None),
        P(None, ("dp", "seq")),
        P(("dp", "seq")),
        P(("dp", "seq")),
        P(None, ("dp", "seq")),
        P(("dp", "seq")),
        P(),
        P(),
        P(),
    )
    return jax.shard_map(
        on_device, mesh=mesh, in_specs=in_specs, out_specs=out_specs, check_vma=False
    )
```

```python
import functools

import jax
import jax.numpy as jnp
from jax import lax
from jax.experimental import pallas as pl
from jax.experimental.pallas import tpu as pltpu
from jax.sharding import PartitionSpec as P

HEADS = 32
HEAD_DIM = 64
STATE = 128
CONV = 4
INNER = 2048
CONV_CH = 2304


epsilon = 1e-05
highest = lax.Precision.HIGH


def from_behind(value, axis, steps):
    count = lax.axis_size(axis)
    leading, last = (max(0, -steps), min(count, count - steps))
    return lax.ppermute(value, axis, [(source, source + steps) for source in range(leading, last)])


def convolve(padded, conv_weight, conv_bias):
    taps = conv_weight.shape[0]
    length = padded.shape[-2] - taps + 1
    total = conv_bias
    for index in range(taps):
        total = total + conv_weight[index] * lax.slice_in_dim(
            padded, index, index + length, axis=padded.ndim - 2
        )
    return total


def bits_of(count):
    return count.bit_length() - 1


def can_pair(shapes, rows):
    return all(size & (size - 1) == 0 for size in shapes) and rows % 16 == 0


def bit_orders(total):
    rest = list(range(1, total))
    return [[0] + rest[i : i + 1] + rest[:i] + rest[i + 1 :] for i in (0, 1, 2, 0)]


class Place:
    def __init__(self, dp, seq):
        self.dp, self.seq = lax.axis_index("dp"), lax.axis_index("seq")
        self.low, self.total = bits_of(seq), bits_of(seq) + bits_of(dp)
        self.owner = self.dp * seq + self.seq

    def bit(self, b):
        return lax.rem(self.owner // 2**b, 2)

    def partner(self, b):
        step = 1 - 2 * self.bit(b)
        if b < self.low:
            return (self.dp, self.seq + step * 2**b)
        return (self.dp + step * 2 ** (b - self.low), self.seq)

    def flipped(self, pairs):
        total = self.owner
        for b, flag in pairs:
            total = total + flag * (1 - 2 * self.bit(b)) * 2**b
        return total

    def greet(self):
        barrier = pltpu.get_barrier_semaphore()
        for b in range(self.total):
            pl.semaphore_signal(
                barrier, inc=1, device_id=self.partner(b), device_id_type=pl.DeviceIdType.MESH
            )
        pl.semaphore_wait(barrier, self.total)


def remote(src, dst, send, recv, device):
    return pltpu.make_async_remote_copy(
        src_ref=src,
        dst_ref=dst,
        send_sem=send,
        recv_sem=recv,
        device_id=device,
        device_id_type=pl.DeviceIdType.MESH,
    )


def gather_kernel(dp, seq, count, *refs):
    ins, outs = refs[:count], refs[count : 2 * count]
    send, recv, own = refs[2 * count :]
    place = Place(dp, seq)
    n = place.total
    orders = [order[::-1] for order in bit_orders(n)]
    locals_ = []
    for s in range(count):
        copy = pltpu.make_async_copy(ins[s], outs[s].at[place.owner], own.at[s])
        copy.start()
        locals_.append(copy)
    place.greet()

    def copy_of(s, held, src, stage):
        order = orders[s]
        owner = place.flipped([(order[i], lax.rem(held // 2**i, 2)) for i in range(stage)])
        slot = 2**stage - 1 + held
        source = src if src is not None else outs[s].at[owner]
        return remote(
            source, outs[s].at[owner], send.at[s, slot], recv.at[s, slot], place.partner(order[stage])
        )

    for stage in range(n - 1, -1, -1):
        for s in range(count):
            copy_of(s, 0, ins[s], stage).start()
    for stage in range(n):

        def arrived(j, carry, stage=stage):
            for s in range(count):
                copy_of(s, j, None, stage).wait_recv()
                for later in range(n - 1, stage, -1):
                    copy_of(s, 2**stage + j, None, later).start()
            return carry

        lax.fori_loop(0, 2**stage, arrived, 0)
    for stage in range(n):

        def sent(j, carry, stage=stage):
            for s in range(count):
                copy_of(s, j, None, stage).wait_send()
            return carry

        lax.fori_loop(0, 2**stage, sent, 0)
    for copy in locals_:
        copy.wait()


def gather_blocks(blocks, dp, seq):
    count, owners = len(blocks), dp * seq
    return pl.pallas_call(
        functools.partial(gather_kernel, dp, seq, count),
        out_shape=[jax.ShapeDtypeStruct((owners,) + b.shape, b.dtype) for b in blocks],
        in_specs=[pl.BlockSpec(memory_space=pltpu.VMEM)] * count,
        out_specs=[pl.BlockSpec(memory_space=pltpu.VMEM)] * count,
        scratch_shapes=[
            pltpu.SemaphoreType.DMA((count, owners)),
            pltpu.SemaphoreType.DMA((count, owners)),
            pltpu.SemaphoreType.DMA((count,)),
        ],
        compiler_params=pltpu.CompilerParams(
            collective_id=0, has_side_effects=True, vmem_limit_bytes=56 * 2**20
        ),
    )(*blocks)


def reduce_kernel(dp, seq, count, *refs):
    ins, outs = refs[:count], refs[count : 2 * count]
    boxes, sums = refs[2 * count : 3 * count], refs[3 * count : 4 * count]
    send, recv = refs[4 * count :]
    place = Place(dp, seq)
    n = place.total
    half0 = 2 ** (n - 1)
    orders = bit_orders(n)
    place.greet()

    def block_of(s, j, mine):
        order = orders[s]
        pairs = [(order[i], 1 - lax.rem(j // 2 ** (n - 1 - i), 2)) for i in range(1, n)]
        return place.flipped(pairs + [(order[0], 0 if mine else 1)])

    def copy_of(s, j, stage):
        half = half0 // 2**stage
        slot = 2 * half0 - 2 * half + j
        if stage == 0:
            source = ins[s].at[block_of(s, j, False)]
        else:
            source = sums[s].at[half0 - 2 * half + j]
        return remote(
            source,
            boxes[s].at[slot],
            send.at[s, slot],
            recv.at[s, slot],
            place.partner(orders[s][stage]),
        )

    def begin(j, carry):
        for s in range(count):
            copy_of(s, j, 0).start()
        return carry

    lax.fori_loop(0, half0, begin, 0)
    for stage in range(n):
        half = half0 // 2**stage

        def add(s, j, stage, half):
            slot = 2 * half0 - 2 * half + j
            here = half0 - half + j
            rows, columns = outs[s].shape
            wide = 512 if columns > 512 else columns
            for start in range(0, columns, wide):
                part = pl.ds(start, min(wide, columns - start))
                if stage == 0:
                    kept = ins[s][block_of(s, j, True), :, part]
                else:
                    kept = sums[s][here, :, part]
                total = kept.astype(jnp.float32) + boxes[s][slot, :, part].astype(jnp.float32)
                if stage == n - 1:
                    outs[s][:, part] = total
                else:
                    sums[s][here, :, part] = total.astype(sums[s].dtype)

        def forward(j, carry, stage=stage, half=half):
            for s in range(count):
                copy_of(s, j, stage).wait_recv()
                add(s, j, stage, half)
                copy_of(s, j, stage + 1).start()
            return carry

        def keep(j, carry, stage=stage, half=half):
            for s in range(count):
                copy_of(s, j, stage).wait_recv()
                add(s, j, stage, half)
            return carry

        if stage < n - 1:
            lax.fori_loop(0, half // 2, forward, 0)
            lax.fori_loop(half // 2, half, keep, 0)
        else:
            keep(0, 0)
    for stage in range(n):

        def sent(j, carry, stage=stage):
            for s in range(count):
                copy_of(s, j, stage).wait_send()
            return carry

        lax.fori_loop(0, half0 // 2**stage, sent, 0)


def reduce_blocks(blocks, dp, seq):
    count, owners = len(blocks), dp * seq
    return pl.pallas_call(
        functools.partial(reduce_kernel, dp, seq, count),
        out_shape=[jax.ShapeDtypeStruct(b.shape[1:], jnp.float32) for b in blocks],
        in_specs=[pl.BlockSpec(memory_space=pltpu.VMEM)] * count,
        out_specs=[pl.BlockSpec(memory_space=pltpu.VMEM)] * count,
        scratch_shapes=[pltpu.VMEM(b.shape, b.dtype) for b in blocks]
        + [pltpu.VMEM((owners // 2,) + b.shape[1:], b.dtype) for b in blocks]
        + [pltpu.SemaphoreType.DMA((count, owners)), pltpu.SemaphoreType.DMA((count, owners))],
        compiler_params=pltpu.CompilerParams(
            collective_id=1, has_side_effects=True, vmem_limit_bytes=58 * 2**20
        ),
    )(*blocks)


def outer_kernel(left_ref, right_ref, out_ref):
    out_ref[...] = jnp.dot(
        left_ref[...], right_ref[...], preferred_element_type=jnp.float32
    ).astype(out_ref.dtype)


def outer_product(left, right):
    (rows, tokens), columns = left.shape, right.shape[1]
    tile = 256 if rows % 256 == 0 else rows
    return pl.pallas_call(
        outer_kernel,
        grid=(rows // tile,),
        out_shape=jax.ShapeDtypeStruct((rows, columns), jnp.bfloat16),
        in_specs=[
            pl.BlockSpec((tile, tokens), lambda i: (i, 0)),
            pl.BlockSpec((tokens, columns), lambda i: (0, 0)),
        ],
        out_specs=pl.BlockSpec((tile, columns), lambda i: (i, 0)),
        cost_estimate=pl.CostEstimate(
            flops=2 * rows * tokens * columns,
            bytes_accessed=2 * (rows * tokens + tokens * columns + rows * columns),
            transcendentals=0,
        ),
    )(left, right)


def carry_scan(state, decay, axis, sign):
    count = lax.axis_size(axis)
    within, within_decay = state, decay
    entering, entering_decay = None, None
    width = 1
    while width < count:
        moved = from_behind(within.astype(jnp.bfloat16), axis, sign * width).astype(jnp.float32)
        last = 2 * width >= count
        if not last or entering is None:
            moved_decay = from_behind(within_decay, axis, sign * width)
        if entering is None:
            entering, entering_decay = moved, moved_decay
        else:
            entering = entering + entering_decay[:, :, None, None] * moved
            if not last:
                entering_decay = entering_decay * moved_decay
        if not last:
            within = within + within_decay[:, :, None, None] * moved
            within_decay = within_decay * moved_decay
        width *= 2
    return jnp.zeros_like(state) if entering is None else entering


def front_fn(tail, rim, conv_weight, conv_bias, dt_bias, decay_log):
    conv_in = tail[..., :CONV_CH]
    dt_raw = tail[..., CONV_CH:]
    padded = jnp.concatenate([rim, conv_in], axis=-2)
    conv_out = jax.nn.silu(convolve(padded, conv_weight, conv_bias))
    leading = conv_out.shape[:-1]
    values = conv_out[..., :INNER].reshape(leading + (HEADS, HEAD_DIM))
    in_map = conv_out[..., INNER : INNER + STATE]
    out_map = conv_out[..., INNER + STATE :]
    step = jax.nn.softplus(dt_raw + dt_bias)
    cumulative = jnp.cumsum(step * -jnp.exp(decay_log), axis=1)
    return (values, in_map, out_map, step, cumulative)


def group_state(values, in_map, step, cumulative):
    weights_end = jnp.exp(cumulative[-1][None, :] - cumulative) * step
    state = jnp.einsum("shp,sn->hpn", values * weights_end[:, :, None], in_map, precision=highest)
    return (state, jnp.exp(cumulative[-1]))


def group_output(values, in_map, out_map, step, cumulative, carried, skip_gain):
    length = values.shape[0]
    scores = jnp.dot(out_map, in_map.T, precision=highest)
    causal = jnp.arange(length)[:, None] >= jnp.arange(length)[None, :]
    spread = cumulative[:, None, :] - cumulative[None, :, :]
    decay = jnp.exp(jnp.where(causal[:, :, None], spread, -10000.0))
    mixing = scores[:, :, None] * decay * step[None, :, :]
    inner_part = jnp.einsum("tsh,shp->thp", mixing, values, precision=highest)
    carried_part = (
        jnp.einsum("tn,hpn->thp", out_map, carried, precision=highest)
        * jnp.exp(cumulative)[:, :, None]
    )
    return inner_part + carried_part + skip_gain[None, :, None] * values


def state_fn(values, in_map, step, cumulative):
    return jax.vmap(group_state)(values, in_map, step, cumulative)


def out_fn(values, in_map, out_map, step, cumulative, gate_raw, carried, skip_gain, norm_gain):
    ssd_out = jax.vmap(group_output, in_axes=(0, 0, 0, 0, 0, 0, None))(
        values, in_map, out_map, step, cumulative, carried, skip_gain
    )
    ssd_out = ssd_out.reshape(gate_raw.shape)
    gated = ssd_out * jax.nn.silu(gate_raw)
    inverse = lax.rsqrt(jnp.mean(gated * gated, axis=-1, keepdims=True) + epsilon)
    return gated * inverse * norm_gain


def by_rows(grad, owners):
    return grad.reshape(owners, -1)


def by_columns(grad, owners):
    rows = grad.shape[0]
    return jnp.transpose(grad.reshape(rows, owners, -1), (1, 0, 2)).reshape(owners, -1)


def on_device(
    block_input,
    in_weight,
    out_weight,
    pre_gain,
    norm_gain,
    conv_weight,
    conv_bias,
    dt_bias,
    decay_log,
    skip_gain,
    cotangent,
):
    seq_dev, length, width = block_input.shape
    dp, seq = lax.axis_size("dp"), lax.axis_size("seq")
    owners = dp * seq
    both = ("dp", "seq")
    fast = can_pair((dp, seq), in_weight.shape[0]) and dp * seq > 4
    small_parts = (pre_gain, norm_gain, conv_weight.reshape(-1), conv_bias)
    small_sizes = [part.size for part in small_parts]
    small = jnp.concatenate(small_parts)
    if fast:
        lines = -(-small.size // 2048) * 16
        small = jnp.pad(small, (0, lines * 128 - small.size)).reshape(lines, 128)
        gate_w, tail_w, out_t, small_all = gather_blocks(
            (in_weight[:, :INNER], in_weight[:, INNER:], out_weight.T, small), dp, seq
        )
        gate_w = gate_w.reshape(width, -1)
        tail_w = tail_w.reshape(width, -1)
        out_t = out_t.reshape(width, INNER)
        small_all = small_all.reshape(owners, -1)
    else:
        in_full = lax.all_gather(in_weight, both, axis=0, tiled=True)
        gate_w, tail_w = in_full[:, :INNER], in_full[:, INNER:]
        out_t = lax.all_gather(out_weight.T, both, axis=0, tiled=True)
        small_all = lax.all_gather(small, both, axis=0)
    pieces, start = [], 0
    for size in small_sizes:
        pieces.append(small_all[:, start : start + size])
        start += size
    pre_full, norm_full, conv_b_full = (pieces[i].reshape(-1) for i in (0, 1, 3))
    conv_w_full = jnp.transpose(pieces[2].reshape(owners, CONV, -1), (1, 0, 2)).reshape(CONV, -1)
    pre_float = pre_full.astype(jnp.float32)
    norm_float = norm_full.astype(jnp.float32)
    inputs = block_input.astype(jnp.float32)
    inv_pre = lax.rsqrt(jnp.mean(inputs * inputs, axis=-1, keepdims=True) + epsilon)
    normed = (inputs * inv_pre * pre_float).astype(jnp.bfloat16)
    flat_normed = normed.reshape(seq_dev * length, width)
    gate_raw = jnp.dot(flat_normed, gate_w, preferred_element_type=jnp.float32).reshape(
        seq_dev, length, -1
    )
    tail = jnp.dot(flat_normed, tail_w, preferred_element_type=jnp.float32).reshape(
        seq_dev, length, -1
    )
    conv_in = tail[:, length - (CONV - 1) :, :CONV_CH]
    rim = from_behind(conv_in, "seq", 1)
    front_out, front_pull = jax.vjp(
        front_fn,
        tail,
        rim,
        conv_w_full.astype(jnp.float32),
        conv_b_full.astype(jnp.float32),
        dt_bias,
        decay_log,
    )
    values, in_map, out_map, step, cumulative = front_out
    state_out, state_pull = jax.vjp(state_fn, values, in_map, step, cumulative)
    state, decay = state_out
    carried = carry_scan(state, decay, "seq", 1)
    mixed_float, out_pull = jax.vjp(
        out_fn, values, in_map, out_map, step, cumulative, gate_raw, carried, skip_gain, norm_float
    )
    mixed = mixed_float.astype(jnp.bfloat16)
    flat_mixed = mixed.reshape(seq_dev * length, INNER)
    block_output = (
        inputs
        + jnp.dot(flat_mixed, out_t.T, preferred_element_type=jnp.float32).reshape(
            seq_dev, length, width
        )
    ).astype(jnp.bfloat16)
    flat_grad = cotangent.reshape(seq_dev * length, width)
    mixed_grad = jnp.dot(flat_grad, out_t, preferred_element_type=jnp.float32).reshape(
        seq_dev, length, INNER
    )
    out_w_grad = jnp.dot(flat_grad.T, flat_mixed, preferred_element_type=jnp.float32)
    (
        values_a,
        in_map_a,
        out_map_grad,
        step_a,
        cumul_a,
        gate_grad,
        local_grad,
        skip_grad,
        norm_grad,
    ) = out_pull(mixed_grad)

    later_grad = carry_scan(local_grad, decay, "seq", -1)
    decay_grad = jnp.sum(later_grad * carried, axis=(2, 3))
    values_b, in_map_b, step_b, cumul_b = state_pull((later_grad, decay_grad))
    front_grads = front_pull(
        (
            values_a + values_b,
            in_map_a + in_map_b,
            out_map_grad,
            step_a + step_b,
            cumul_a + cumul_b,
        )
    )
    tail_float, rim_grad, conv_w_grad, conv_b_grad, dt_grad, decay_log_grad = front_grads
    returned = from_behind(rim_grad, "seq", -1)
    tail_float = tail_float + jnp.pad(returned, ((0, 0), (length - (CONV - 1), 0), (0, HEADS)))
    tail_grad = tail_float.astype(jnp.bfloat16).reshape(seq_dev * length, -1)
    gate_grad = gate_grad.astype(jnp.bfloat16).reshape(seq_dev * length, -1)
    gate_w_grad = jnp.dot(flat_normed.T, gate_grad, preferred_element_type=jnp.float32)
    if fast:
        tail_w_grad = outer_product(flat_normed.T, tail_grad)
    else:
        tail_w_grad = jnp.dot(flat_normed.T, tail_grad, preferred_element_type=jnp.float32)
    normed_grad = (
        jnp.dot(gate_grad, gate_w.T, preferred_element_type=jnp.float32)
        + jnp.dot(tail_grad, tail_w.T, preferred_element_type=jnp.float32)
    ).reshape(seq_dev, length, width)
    pre_grad = jnp.sum(normed_grad * inputs * inv_pre, axis=(0, 1))
    scaled = normed_grad * pre_float
    unit = inputs * inv_pre
    input_grad = inv_pre * (
        scaled - unit * jnp.mean(scaled * unit, axis=-1, keepdims=True)
    ) + cotangent.astype(jnp.float32)
    small_grads = jnp.concatenate(
        (
            by_rows(pre_grad, owners),
            by_rows(norm_grad, owners),
            by_columns(conv_w_grad, owners),
            by_rows(conv_b_grad, owners),
        ),
        axis=1,
    )
    heads = jnp.concatenate((dt_grad, decay_log_grad, skip_grad))
    if fast:
        total = small_grads.shape[1] + heads.size
        lines = -(-total // 1024) * 8
        heads_all = jnp.broadcast_to(heads, (owners, heads.size))
        small_grads = jnp.concatenate((small_grads, heads_all), axis=1)
        small_grads = jnp.pad(small_grads, ((0, 0), (0, lines * 128 - total)))
        rows = width // owners
        gate_share, tail_share, out_share, small_share = reduce_blocks(
            (
                gate_w_grad.astype(jnp.bfloat16).reshape(owners, rows, -1),
                tail_w_grad.astype(jnp.bfloat16).reshape(owners, rows, -1),
                out_w_grad.astype(jnp.bfloat16).reshape(owners, rows, -1),
                small_grads.reshape(owners, lines, 128),
            ),
            dp,
            seq,
        )
        small_share = small_share.reshape(-1)
        heads = small_share[total - heads.size : total]
        in_share = jnp.concatenate((gate_share, tail_share), axis=1)
        out_share = out_share.T
    else:
        scatter = functools.partial(
            lax.psum_scatter, axis_name=both, scatter_dimension=0, tiled=True
        )
        in_share = scatter(jnp.concatenate((gate_w_grad, tail_w_grad), axis=1))
        out_share = scatter(out_w_grad).T
        small_share = scatter(small_grads)[0]
        heads = lax.psum(heads, both)
    shares, start = [], 0
    for size in small_sizes:
        shares.append(small_share[start : start + size])
        start += size
    pre_share, norm_share, conv_w_share, conv_b_share = shares
    conv_w_share = conv_w_share.reshape(CONV, -1)
    heads_total = (heads[:HEADS], heads[HEADS : 2 * HEADS], heads[2 * HEADS :])
    return (
        block_output,
        input_grad,
        in_share,
        out_share,
        pre_share,
        norm_share,
        conv_w_share,
        conv_b_share,
        heads_total[0],
        heads_total[1],
        heads_total[2],
    )


def solution(mesh):
    in_specs = (
        P("dp", "seq", None),
        P(("dp", "seq"), None),
        P(None, ("dp", "seq")),
        P(("dp", "seq")),
        P(("dp", "seq")),
        P(None, ("dp", "seq")),
        P(("dp", "seq")),
        P(),
        P(),
        P(),
        P("dp", "seq", None),
    )
    out_specs = (
        P("dp", "seq", None),
        P("dp", "seq", None),
        P(("dp", "seq"), None),
        P(None, ("dp", "seq")),
        P(("dp", "seq")),
        P(("dp", "seq")),
        P(None, ("dp", "seq")),
        P(("dp", "seq")),
        P(),
        P(),
        P(),
    )
    return jax.shard_map(
        on_device, mesh=mesh, in_specs=in_specs, out_specs=out_specs, check_vma=False
    )
```
